1024 devices in a mesh: section: 16 (over y, core), row: 16 (over z), col: 4 (over x).
Axes of the slice: x: 4, y: 8, z: 16, core: 2. Of those that a mesh axis runs over, the one named last changes fastest.
Arguments:
- inputs: bfloat16 [16, 3072, 5120], P('section', 'row', 'col'), may hold values from -12 to 12
- down_weight: bfloat16 [16, 512, 5120], P('section', 'row', 'col'), may hold values from -5 to 5
- up_weight: bfloat16 [16, 512, 8192], P('section', 'row', 'col'), may hold values from -0.25 to 0.25
- value_grad: bfloat16 [16, 3072, 8192], P('section', 'row', 'col'), may hold values from -1.1953125 to 1.1953125
Outputs:
- passed_grad: bfloat16 [16, 3072, 5120], P('section', 'row', 'col')
- down_grad: bfloat16 [16, 512, 5120], P('section', 'row', 'col')
- up_grad: bfloat16 [16, 512, 8192], P('section', 'row', 'col')
The draws below stay inside these ranges and needn't reach their ends.
All inputs are finite; a program needn't handle non-finite values.
Results may differ from the reference program's by a relative error of at most 0.03.
Values may be sent and summed in bfloat16 or wider, within the bound.
A program may use at most 32 MiB of HBM per device.

```python
import math
import jax
import jax.numpy as jnp
from jax import lax

D = 5120
L = 512
TOK_ROW = 192
TOKENS = 3072
FEAT = 8192
SEGMENTS = 16
N_ROW = 16


def draw_inputs(key, part):
    first, second = jax.random.split(key, 2)
    scales = jnp.exp(jax.random.uniform(first, (SEGMENTS, TOKENS, 1), jnp.float32, math.log(0.3), math.log(3.0)))
    values = jnp.clip(jax.random.normal(second, (SEGMENTS, TOKENS, D), jnp.float32), -4.0, 4.0)
    return (values * scales).astype(jnp.bfloat16)


def draw_down_weight(key, part):
    first, second = jax.random.split(key, 2)
    scales = jnp.exp(jax.random.uniform(first, (SEGMENTS, L, 1), jnp.float32, 0.0, math.log(10.0)))
    values = jnp.clip(jax.random.normal(second, (SEGMENTS, L, D), jnp.float32), -4.0, 4.0)
    return (values * scales * (1.0 / math.sqrt(D))).astype(jnp.bfloat16)


def steps_of(stream_key, dims, pieces, smallest, high):
    def one(position, shards_of):
        steps = jax.random.uniform(jax.random.fold_in(jax.random.fold_in(stream_key, 6), position), (shards_of,), jnp.float32, smallest / len(pieces), high / len(pieces))
        return jnp.repeat(jnp.exp(steps), dims[position] // shards_of).reshape((-1,) + (1,) * (len(dims) - position - 1))

    loudness = one(*pieces[0])
    for cut in pieces[1:]:
        loudness = loudness * one(*cut)
    return loudness


def normal_values(rng, dims, deviation, bound, shards=(), kind=jnp.bfloat16):
    drawn = jax.random.normal(rng, dims, jnp.float32) * deviation
    if len(shards) > 0:
        drawn = steps_of(rng, dims, shards, -0.22, 0.18) * drawn
    return jnp.clip(drawn, min=-bound, max=bound).astype(kind)


def setup_inputs(seed: int = 0) -> dict:
    seeds = jax.random.split(jax.random.key(seed), 5)
    return {
        "inputs": draw_inputs(jax.random.fold_in(seeds[4], 71), 0),
        "down_weight": draw_down_weight(jax.random.fold_in(seeds[4], 71), 0),
        "up_weight": normal_values(seeds[2], (SEGMENTS, L, FEAT), L ** -0.5, 0.25, ((0, 16), (1, 16), (2, 4))),
        "value_grad": normal_values(seeds[3], (SEGMENTS, TOKENS, FEAT), 0.2, 1.1953125, ((0, 16), (1, 16), (2, 4))),
    }


def block_sum(left, right):
    left_blocks = left.reshape(N_ROW, TOK_ROW, left.shape[1]).astype(jnp.float32)
    right_blocks = right.reshape(N_ROW, TOK_ROW, right.shape[1]).astype(jnp.float32)
    terms = jnp.einsum('btl,btf->blf', left_blocks, right_blocks)
    rounded = lax.optimization_barrier(terms.astype(jnp.bfloat16))
    return lax.optimization_barrier(jnp.sum(rounded.astype(jnp.float32), axis=0)).astype(jnp.bfloat16)

def segment_grads(operands):
    inputs, down_weight, up_weight, value_grad = operands
    latent = jnp.dot(inputs, down_weight.T, preferred_element_type=jnp.float32)
    inv_rms = lax.rsqrt(lax.optimization_barrier(jnp.mean(latent * latent, axis=-1, keepdims=True)) + 1e-06)
    normed = latent * inv_rms
    normed_bf = normed.astype(jnp.bfloat16)
    normed_grad = jnp.dot(value_grad, up_weight.T, preferred_element_type=jnp.float32)
    up_grad = block_sum(normed_bf, value_grad)
    inner = lax.optimization_barrier(jnp.mean(normed_grad * normed, axis=-1, keepdims=True))
    latent_grad = inv_rms * (normed_grad - normed * inner)
    latent_bf = latent_grad.astype(jnp.bfloat16)
    down_grad = block_sum(latent_bf, inputs)
    input_grad = jnp.dot(latent_bf, down_weight, preferred_element_type=jnp.float32).astype(jnp.bfloat16)
    return (input_grad, down_grad, up_grad)

def reference(inputs, down_weight, up_weight, value_grad):
    input_grad, down_grad, up_grad = lax.map(segment_grads, (inputs, down_weight, up_weight, value_grad))
    filler = jnp.zeros((1, TOKENS, D), jnp.bfloat16)
    passed_grad = jnp.concatenate([input_grad[1:], filler], axis=0)
    return (passed_grad, down_grad, up_grad)
```

```python
import functools

import jax
import jax.numpy as jnp
from jax import lax
from jax.experimental import pallas as pl
from jax.experimental.pallas import tpu as pltpu
from jax.sharding import PartitionSpec as P

MESH = pl.DeviceIdType.MESH
F32 = jnp.float32
BF16 = jnp.bfloat16


def remote(src, dst, send, recv, device):
    return pltpu.make_async_remote_copy(
        src_ref=src, dst_ref=dst, send_sem=send, recv_sem=recv, device_id=device, device_id_type=MESH
    )


class Stream:
    def __init__(self, names, half, block, width):
        self.__dict__.update(names)
        self.half, self.block, self.width = half, block, width


def kernel(n_sec, n_row, n_col, *refs):
    (x_hbm, dw_hbm, uw_hbm, v_hbm, passed_ref, dg_ref, ug_ref) = refs[:7]
    (xs, vs, xt, vt, wd, wu, pd, pu, qd, qu, normed, nb, lb, sd, su, rd, ru, own_d, own_u, ig, zero,
     load_sem, ag_send_d, ag_recv_d, ag_send_u, ag_recv_u, x_send_d, x_recv_d, x_send_u, x_recv_u,
     rs_send_d, rs_recv_d, rs_send_u, rs_recv_u, sec_send, sec_recv, zero_sem) = refs[7:]
    half_ring = n_row // 2
    block = dw_hbm.shape[1]
    latents = n_row * block
    sec, row, col = lax.axis_index("section"), lax.axis_index("row"), lax.axis_index("col")
    right = {"row": lax.rem(row + 1, n_row)}
    left = {"row": lax.rem(row + n_row - 1, n_row)}
    peers = [{"col": lax.rem(col + j, n_col)} for j in range(1, n_col)]
    down = {"section": lax.rem(sec + n_sec - 1, n_sec)}
    up = {"section": lax.rem(sec + 1, n_sec)}

    loads = [
        pltpu.make_async_copy(dw_hbm.at[0], wd.at[0, 0:block], load_sem.at[0]),
        pltpu.make_async_copy(uw_hbm.at[0], wu.at[0, 0:block], load_sem.at[1]),
        pltpu.make_async_copy(x_hbm.at[0], xs, load_sem.at[2]),
        pltpu.make_async_copy(v_hbm.at[0], vs, load_sem.at[3]),
    ]
    for load in loads:
        load.start()
    barrier = pltpu.get_barrier_semaphore()
    for device in [right, left, down, up] + peers:
        pl.semaphore_signal(barrier, inc=1, device_id=device, device_id_type=MESH)
    pl.semaphore_wait(barrier, 4 + len(peers))
    loads[0].wait()
    loads[1].wait()

    d = Stream(dict(w=wd, at=xt, a=xs, p=pd, q=qd, lat=lb, s=sd, r=rd, own=own_d, out=dg_ref,
                    ag_send=ag_send_d, ag_recv=ag_recv_d, x_send=x_send_d, x_recv=x_recv_d,
                    rs_send=rs_send_d, rs_recv=rs_recv_d), half_ring, block, dw_hbm.shape[2])
    u = Stream(dict(w=wu, at=vt, a=vs, p=pu, q=qu, lat=nb, s=su, r=ru, own=own_u, out=ug_ref,
                    ag_send=ag_send_u, ag_recv=ag_recv_u, x_send=x_send_u, x_recv=x_recv_u,
                    rs_send=rs_send_u, rs_recv=rs_recv_u), half_ring, block, uw_hbm.shape[2])
    lo, hi = slice(0, block), slice(block, 2 * block)

    def gather_copies(t, k):
        from_lo = t.w.at[k, lo]
        from_hi = t.w.at[k, lo if isinstance(k, int) and k == 0 else hi]
        return (
            remote(from_lo, t.w.at[k + 1, lo], t.ag_send.at[0, k], t.ag_recv.at[0, k], right),
            remote(from_hi, t.w.at[k + 1, hi], t.ag_send.at[1, k], t.ag_recv.at[1, k], left),
        )

    def gather_last(t):
        k, cut = half_ring - 1, t.width // 2
        return (
            remote(t.w.at[k, lo, 0:cut], t.w.at[0, hi, 0:cut], t.ag_send.at[0, k], t.ag_recv.at[0, k], right),
            remote(t.w.at[k, hi, cut:], t.w.at[0, hi, cut:], t.ag_send.at[1, k], t.ag_recv.at[1, k], left),
        )

    def exchange(t, k):
        for j, peer in enumerate(peers):
            remote(t.p.at[k], t.q.at[j, k], t.x_send, t.x_recv, peer).start()

    def partial_latents(t, k):
        t.p[k] = jnp.dot(t.w[k], t.at[...], preferred_element_type=F32).astype(BF16)
        exchange(t, k)

    def gather_step(t, k, last):
        arrived = gather_copies(t, k - 1)
        onward = gather_last(t) if last else gather_copies(t, k)
        for before, after in zip(arrived, onward):
            before.wait_recv()
            after.start()
        partial_latents(t, k)

    def finish_gather(t):
        for copy in gather_last(t):
            copy.wait_recv()
        partial_latents(t, 0)

    for t in (d, u):
        for copy in gather_copies(t, 0):
            copy.start()
    for t in (d, u):
        cut = t.width // 2
        t.r[0, lo, 0:cut] = jnp.zeros((block, cut), BF16)
        t.r[0, hi, cut:] = jnp.zeros((block, cut), BF16)
    zero[...] = jnp.zeros_like(zero)
    loads[2].wait()
    xt[...] = xs[...].T
    loads[3].wait()
    vt[...] = vs[...].T

    @pl.loop(1, half_ring - 1)
    def _(k):
        gather_step(d, k, False)
        gather_step(u, k, False)

    gather_step(d, half_ring - 1, True)
    gather_step(u, half_ring - 1, True)
    finish_gather(d)
    finish_gather(u)

    def exchanged(t):
        pltpu.make_async_copy(t.q, t.q, t.x_recv).wait()
        total = t.p[...].astype(F32)
        for j in range(len(peers)):
            total = total + t.q[j].astype(F32)
        return total.reshape(latents, total.shape[-1])

    latent = exchanged(d)
    inv_rms = lax.rsqrt(jnp.sum(latent * latent, axis=0, keepdims=True) * (1.0 / latents) + 1e-6)
    value = latent * inv_rms
    nb[...] = value.astype(BF16)
    normed[...] = value

    def scatter_first(t):
        cut = t.width // 2
        return (
            remote(t.s.at[0, hi, 0:cut], t.r.at[0, hi, 0:cut], t.rs_send.at[0, 0], t.rs_recv.at[0, 0], right),
            remote(t.s.at[0, hi, cut:], t.r.at[0, lo, cut:], t.rs_send.at[1, 0], t.rs_recv.at[1, 0], left),
        )

    def scatter_copies(t, j):
        pair = half_ring - j
        return (
            remote(t.s.at[pair, hi], t.r.at[j, hi], t.rs_send.at[0, j], t.rs_recv.at[0, j], right),
            remote(t.s.at[pair, lo], t.r.at[j, lo], t.rs_send.at[1, j], t.rs_recv.at[1, j], left),
        )

    def product(t, pair):
        rows = pl.ds(pl.multiple_of(pair * 2 * block, 2 * block), 2 * block)
        return jnp.dot(t.lat[rows, :], t.a[...], preferred_element_type=F32)

    def scatter_start(t):
        both = product(t, 0)
        t.s[0] = both.astype(BF16)
        for copy in scatter_first(t):
            copy.start()

    def scatter_step(t, j, first):
        t.s[half_ring - j] = product(t, half_ring - j).astype(BF16)
        arrived = scatter_first(t) if first else scatter_copies(t, j - 1)
        for part, before, after in zip((hi, lo), arrived, scatter_copies(t, j)):
            before.wait_recv()
            t.s[half_ring - j, part] = (
                t.s[half_ring - j, part].astype(F32) + t.r[j - 1, part].astype(F32)
            ).astype(BF16)
            after.start()

    def scatter_end(t):
        for copy in scatter_copies(t, half_ring - 1):
            copy.wait_recv()
        last = half_ring - 1
        t.out[0] = (
            t.s[0, lo].astype(F32) + t.r[last, lo].astype(F32) + t.r[last, hi].astype(F32)
        ).astype(BF16)

    scatter_start(u)

    normed_grad = exchanged(u)
    value = normed[...]
    inner = jnp.sum(normed_grad * value, axis=0, keepdims=True) * (1.0 / latents)
    lat_grad = inv_rms * (normed_grad - value * inner)
    lb[...] = lat_grad.astype(BF16)
    scatter_start(d)

    scatter_step(u, 1, True)
    scatter_step(d, 1, True)
    ig[...] = jnp.dot(
        lb[...].T, wd[...].reshape(latents, d.width), preferred_element_type=F32
    ).astype(BF16)
    to_section = remote(ig, passed_ref.at[0], sec_send, sec_recv, down)
    fill = pltpu.make_async_copy(zero, passed_ref.at[0], zero_sem)

    @pl.when(sec > 0)
    def _():
        to_section.start()

    @pl.when(sec == n_sec - 1)
    def _():
        fill.start()

    @pl.loop(2, half_ring)
    def _(j):
        scatter_step(u, j, False)
        scatter_step(d, j, False)

    scatter_end(u)
    scatter_end(d)

    @pl.when(sec > 0)
    def _():
        to_section.wait_send()

    @pl.when(sec < n_sec - 1)
    def _():
        to_section.wait_recv()

    @pl.when(sec == n_sec - 1)
    def _():
        fill.wait()

    for t in (d, u):
        pltpu.make_async_copy(t.q, t.q, t.x_send).wait()
        for copy in gather_copies(t, 0) + gather_last(t) + scatter_first(t):
            copy.wait_send()

        @pl.loop(1, half_ring - 1)
        def _(k):
            for copy in gather_copies(t, k):
                copy.wait_send()

        @pl.loop(1, half_ring)
        def _(j):
            for copy in scatter_copies(t, j):
                copy.wait_send()


def body(n_sec, n_row, n_col, inputs, down_weight, up_weight, value_grad):
    _, tokens, width = inputs.shape
    _, block, feat = up_weight.shape
    half = n_row // 2
    latents = n_row * block
    pair = 2 * block
    dma = pltpu.SemaphoreType.DMA
    out = lambda shape: jax.ShapeDtypeStruct(shape, BF16)
    return tuple(pl.pallas_call(
        functools.partial(kernel, n_sec, n_row, n_col),
        out_shape=(out(inputs.shape), out(down_weight.shape), out(up_weight.shape)),
        in_specs=[pl.BlockSpec(memory_space=pl.ANY)] * 4,
        out_specs=(
            pl.BlockSpec(memory_space=pl.ANY),
            pl.BlockSpec(memory_space=pltpu.VMEM),
            pl.BlockSpec(memory_space=pltpu.VMEM),
        ),
        scratch_shapes=[
            pltpu.VMEM((tokens, width), BF16),
            pltpu.VMEM((tokens, feat), BF16),
            pltpu.VMEM((width, tokens), BF16),
            pltpu.VMEM((feat, tokens), BF16),
            pltpu.VMEM((half, pair, width), BF16),
            pltpu.VMEM((half, pair, feat), BF16),
            pltpu.VMEM((half, pair, tokens), BF16),
            pltpu.VMEM((half, pair, tokens), BF16),
            pltpu.VMEM((n_col - 1, half, pair, tokens), BF16),
            pltpu.VMEM((n_col - 1, half, pair, tokens), BF16),
            pltpu.VMEM((latents, tokens), F32),
            pltpu.VMEM((latents, tokens), BF16),
            pltpu.VMEM((latents, tokens), BF16),
            pltpu.VMEM((half, pair, width), BF16),
            pltpu.VMEM((half, pair, feat), BF16),
            pltpu.VMEM((half, pair, width), BF16),
            pltpu.VMEM((half, pair, feat), BF16),
            pltpu.VMEM((block, width), F32),
            pltpu.VMEM((block, feat), F32),
            pltpu.VMEM((tokens, width), BF16),
            pltpu.VMEM((tokens, width), BF16),
            dma((4,)),
            dma((2, half)), dma((2, half)), dma((2, half)), dma((2, half)),
            dma, dma, dma, dma,
            dma((2, half)), dma((2, half)), dma((2, half)), dma((2, half)),
            dma, dma, dma,
        ],
        compiler_params=pltpu.CompilerParams(
            collective_id=0, has_side_effects=True, vmem_limit_bytes=48 * 1024 * 1024
        ),
    )(inputs, down_weight, up_weight, value_grad))


def solution(mesh):
    spec = P("section", "row", "col")
    sizes = (mesh.shape["section"], mesh.shape["row"], mesh.shape["col"])
    return jax.shard_map(
        functools.partial(body, *sizes),
        mesh=mesh,
        in_specs=(spec,) * 4,
        out_specs=(spec,) * 3,
        check_vma=False,
    )
```

```python
import functools

import jax
import jax.numpy as jnp
from jax import lax
from jax.experimental import pallas as pl
from jax.experimental.pallas import tpu as pltpu
from jax.sharding import PartitionSpec as P

MESH = pl.DeviceIdType.MESH
F32 = jnp.float32
BF16 = jnp.bfloat16


def remote(src, dst, send, recv, device):
    return pltpu.make_async_remote_copy(
        src_ref=src, dst_ref=dst, send_sem=send, recv_sem=recv, device_id=device, device_id_type=MESH
    )


class Stream:
    def __init__(self, **refs):
        self.__dict__.update(refs)


class Chain:
    def __init__(self, stream, index, begin, end):
        self.w, self.s, self.r = stream.w, stream.s, stream.r
        self.left_part, self.right_part = slice(begin, (begin + end) // 2), slice((begin + end) // 2, end)
        self.columns = slice(begin, end)
        self.gather_send, self.gather_recv, self.scatter_send, self.scatter_recv = (
            sem.at[index] for sem in stream.sems
        )


def kernel(n_sec, n_row, n_col, *refs):
    (x_hbm, dw_hbm, uw_hbm, v_hbm, passed_ref, dg_ref, ug_ref) = refs[:7]
    (xs, vs, xt, vt, wd, wu, pd, pu, qd, qu, normed, nb, lb, sd, su, rd, ru, ig, zero, load_sem,
     gather_send, gather_recv, scatter_send, scatter_recv, x_send, x_recv, sec_send, sec_recv, zero_sem) = refs[7:]
    half_ring = n_row // 2
    block = dw_hbm.shape[1]
    latents = n_row * block
    sec, row, col = lax.axis_index("section"), lax.axis_index("row"), lax.axis_index("col")
    right = {"row": lax.rem(row + 1, n_row)}
    left = {"row": lax.rem(row + n_row - 1, n_row)}
    peers = [{"col": lax.rem(col + j, n_col)} for j in range(1, n_col)]
    down = {"section": lax.rem(sec + n_sec - 1, n_sec)}
    up = {"section": lax.rem(sec + 1, n_sec)}

    loads = [
        pltpu.make_async_copy(dw_hbm.at[0], wd.at[0, 0:block], load_sem.at[0]),
        pltpu.make_async_copy(uw_hbm.at[0], wu.at[0, 0:block], load_sem.at[1]),
        pltpu.make_async_copy(x_hbm.at[0], xs, load_sem.at[2]),
        pltpu.make_async_copy(v_hbm.at[0], vs, load_sem.at[3]),
    ]
    for load in loads:
        load.start()
    barrier = pltpu.get_barrier_semaphore()
    for device in [right, left, down, up] + peers:
        pl.semaphore_signal(barrier, inc=1, device_id=device, device_id_type=MESH)
    pl.semaphore_wait(barrier, 4 + len(peers))
    loads[0].wait()
    loads[1].wait()

    sems = (gather_send, gather_recv, scatter_send, scatter_recv)
    d = Stream(w=wd, at=xt, a=xs, p=pd, q=qd, lat=lb, s=sd, r=rd, out=dg_ref, sems=sems,
               x_send=x_send.at[0], x_recv=x_recv.at[0])
    u = Stream(w=wu, at=vt, a=vs, p=pu, q=qu, lat=nb, s=su, r=ru, out=ug_ref, sems=sems,
               x_send=x_send.at[1], x_recv=x_recv.at[1])
    width, feat = xs.shape[1], vs.shape[1]
    d.chains = [Chain(d, 0, 0, width)]
    u.chains = [Chain(u, 1, 0, feat // 2), Chain(u, 2, feat // 2, feat)]
    chains = d.chains + u.chains
    lo, hi = slice(0, block), slice(block, 2 * block)

    def gather_copies(c, k):
        from_hi = lo if isinstance(k, int) and k == 0 else hi
        return (
            remote(c.w.at[k, lo, c.columns], c.w.at[k + 1, lo, c.columns],
                   c.gather_send.at[0, k], c.gather_recv.at[0, k], right),
            remote(c.w.at[k, from_hi, c.columns], c.w.at[k + 1, hi, c.columns],
                   c.gather_send.at[1, k], c.gather_recv.at[1, k], left),
        )

    def gather_last(c):
        k = half_ring - 1
        return (
            remote(c.w.at[k, lo, c.left_part], c.w.at[0, hi, c.left_part],
                   c.gather_send.at[0, k], c.gather_recv.at[0, k], right),
            remote(c.w.at[k, hi, c.right_part], c.w.at[0, hi, c.right_part],
                   c.gather_send.at[1, k], c.gather_recv.at[1, k], left),
        )

    def pass_on(c, k):
        last = isinstance(k, int) and k == half_ring - 1
        for before, after in zip(gather_copies(c, k - 1), gather_last(c) if last else gather_copies(c, k)):
            before.wait_recv()
            after.start()

    def arrive_last(c):
        for copy in gather_last(c):
            copy.wait_recv()

    def partial_latents(t, k):
        t.p[k] = jnp.dot(t.w[k], t.at[...], preferred_element_type=F32).astype(BF16)
        for j, peer in enumerate(peers):
            remote(t.p.at[k], t.q.at[j, k], t.x_send, t.x_recv, peer).start()

    def exchanged(t):
        pltpu.make_async_copy(t.q, t.q, t.x_recv).wait()
        total = t.p[...].astype(F32)
        for j in range(len(peers)):
            total = total + t.q[j].astype(F32)
        return total.reshape(latents, total.shape[-1])

    def scatter_first(c):
        return (
            remote(c.s.at[0, hi, c.left_part], c.r.at[0, hi, c.left_part],
                   c.scatter_send.at[0, 0], c.scatter_recv.at[0, 0], right),
            remote(c.s.at[0, hi, c.right_part], c.r.at[0, lo, c.right_part],
                   c.scatter_send.at[1, 0], c.scatter_recv.at[1, 0], left),
        )

    def scatter_copies(c, j):
        pair = half_ring - j
        return (
            remote(c.s.at[pair, hi, c.columns], c.r.at[j, hi, c.columns],
                   c.scatter_send.at[0, j], c.scatter_recv.at[0, j], right),
            remote(c.s.at[pair, lo, c.columns], c.r.at[j, lo, c.columns],
                   c.scatter_send.at[1, j], c.scatter_recv.at[1, j], left),
        )

    def product(t, pair):
        rows = slice(pair * 2 * block, (pair + 1) * 2 * block)
        t.s[pair] = jnp.dot(t.lat[rows, :], t.a[...], preferred_element_type=F32).astype(BF16)

    def scatter_start(t):
        product(t, 0)
        for c in t.chains:
            for copy in scatter_first(c):
                copy.start()

    def scatter_step(t, j):
        pair = half_ring - j
        product(t, pair)
        for c in t.chains:
            arrived = scatter_first(c) if j == 1 else scatter_copies(c, j - 1)
            for part, before, after in zip((hi, lo), arrived, scatter_copies(c, j)):
                before.wait_recv()
                t.s[pair, part, c.columns] = (
                    t.s[pair, part, c.columns].astype(F32) + t.r[j - 1, part, c.columns].astype(F32)
                ).astype(BF16)
                after.start()

    def scatter_end(t):
        last = half_ring - 1
        for c in t.chains:
            for copy in scatter_copies(c, last):
                copy.wait_recv()
        t.out[0] = (
            t.s[0, lo].astype(F32) + t.r[last, lo].astype(F32) + t.r[last, hi].astype(F32)
        ).astype(BF16)

    for c in chains:
        for copy in gather_copies(c, 0):
            copy.start()
    for c in chains:
        c.r[0, lo, c.left_part] = jnp.zeros((block, c.left_part.stop - c.left_part.start), BF16)
        c.r[0, hi, c.right_part] = jnp.zeros((block, c.right_part.stop - c.right_part.start), BF16)
    zero[...] = jnp.zeros_like(zero)
    loads[2].wait()
    xt[...] = xs[...].T
    loads[3].wait()
    vt[...] = vs[...].T

    ahead = (half_ring - 2) // 2

    @pl.loop(1, ahead + 1)
    def _(i):
        pass_on(d.chains[0], 2 * i - 1)
        partial_latents(d, 2 * i - 1)
        pass_on(u.chains[0], i)
        pass_on(d.chains[0], 2 * i)
        partial_latents(d, 2 * i)
        pass_on(u.chains[1], i)
        partial_latents(u, i)

    def up_gather(k):
        for c in u.chains:
            pass_on(c, k)
        partial_latents(u, k)

    pass_on(d.chains[0], half_ring - 1)
    partial_latents(d, half_ring - 1)
    rest = list(range(ahead + 1, half_ring))
    if len(rest) > 1:
        up_gather(rest.pop(0))
    arrive_last(d.chains[0])
    partial_latents(d, 0)
    if len(rest) > 2:
        up_gather(rest.pop(0))

    latent = exchanged(d)
    inv_rms = lax.rsqrt(jnp.sum(latent * latent, axis=0, keepdims=True) * (1.0 / latents) + 1e-6)
    value = latent * inv_rms
    nb[...] = value.astype(BF16)
    normed[...] = value

    if len(rest) > 1:
        up_gather(rest.pop(0))
    scatter_start(u)
    for k in rest:
        up_gather(k)
    scatter_step(u, 1)
    for c in u.chains:
        arrive_last(c)
    partial_latents(u, 0)
    up_steps, down_steps = list(range(2, half_ring)), list(range(1, half_ring))
    if len(up_steps) > 1:
        scatter_step(u, up_steps.pop(0))

    normed_grad = exchanged(u)
    value = normed[...]
    inner = jnp.sum(normed_grad * value, axis=0, keepdims=True) * (1.0 / latents)
    lat_grad = inv_rms * (normed_grad - value * inner)
    lb[...] = lat_grad.astype(BF16)
    scatter_start(d)
    if len(up_steps) > 1:
        scatter_step(u, up_steps.pop(0))
    scatter_step(d, down_steps.pop(0))

    ig[...] = jnp.dot(
        lb[...].T, wd[...].reshape(latents, width), preferred_element_type=F32
    ).astype(BF16)
    to_section = remote(ig, passed_ref.at[0], sec_send, sec_recv, down)
    fill = pltpu.make_async_copy(zero, passed_ref.at[0], zero_sem)

    @pl.when(sec > 0)
    def _():
        to_section.start()

    @pl.when(sec == n_sec - 1)
    def _():
        fill.start()

    while up_steps or down_steps:
        if len(down_steps) > len(up_steps) and down_steps:
            scatter_step(d, down_steps.pop(0))
        if up_steps:
            scatter_step(u, up_steps.pop(0))
        if down_steps:
            scatter_step(d, down_steps.pop(0))

    scatter_end(u)
    scatter_end(d)

    @pl.when(sec > 0)
    def _():
        to_section.wait_send()

    @pl.when(sec < n_sec - 1)
    def _():
        to_section.wait_recv()

    @pl.when(sec == n_sec - 1)
    def _():
        fill.wait()

    for t in (d, u):
        pltpu.make_async_copy(t.q, t.q, t.x_send).wait()
    for c in chains:
        for copy in gather_copies(c, 0) + gather_last(c) + scatter_first(c):
            copy.wait_send()

        @pl.loop(1, half_ring - 1)
        def _(k):
            for copy in gather_copies(c, k):
                copy.wait_send()

        @pl.loop(1, half_ring)
        def _(j):
            for copy in scatter_copies(c, j):
                copy.wait_send()


def hand_over(*refs):
    n = (len(refs) - 1) // 2
    copies = [pltpu.make_async_copy(refs[i], refs[n + i], refs[-1].at[i]) for i in range(n)]
    for copy in copies:
        copy.start()
    for copy in copies:
        copy.wait()


def body(n_sec, n_row, n_col, inputs, down_weight, up_weight, value_grad):
    _, tokens, width = inputs.shape
    _, block, feat = up_weight.shape
    half = n_row // 2
    latents = n_row * block
    pair = 2 * block
    dma = pltpu.SemaphoreType.DMA
    out = lambda shape: jax.ShapeDtypeStruct(shape, BF16)
    hbm = pl.BlockSpec(memory_space=pltpu.HBM)
    results = pl.pallas_call(
        functools.partial(kernel, n_sec, n_row, n_col),
        out_shape=(out(inputs.shape), out(down_weight.shape), out(up_weight.shape)),
        in_specs=[hbm] * 4,
        out_specs=(
            hbm,
            pl.BlockSpec(memory_space=pltpu.VMEM),
            pl.BlockSpec(memory_space=pltpu.VMEM),
        ),
        scratch_shapes=[
            pltpu.VMEM((tokens, width), BF16),
            pltpu.VMEM((tokens, feat), BF16),
            pltpu.VMEM((width, tokens), BF16),
            pltpu.VMEM((feat, tokens), BF16),
            pltpu.VMEM((half, pair, width), BF16),
            pltpu.VMEM((half, pair, feat), BF16),
            pltpu.VMEM((half, pair, tokens), BF16),
            pltpu.VMEM((half, pair, tokens), BF16),
            pltpu.VMEM((n_col - 1, half, pair, tokens), BF16),
            pltpu.VMEM((n_col - 1, half, pair, tokens), BF16),
            pltpu.VMEM((latents, tokens), F32),
            pltpu.VMEM((latents, tokens), BF16),
            pltpu.VMEM((latents, tokens), BF16),
            pltpu.VMEM((half, pair, width), BF16),
            pltpu.VMEM((half, pair, feat), BF16),
            pltpu.VMEM((half, pair, width), BF16),
            pltpu.VMEM((half, pair, feat), BF16),
            pltpu.VMEM((tokens, width), BF16),
            pltpu.VMEM((tokens, width), BF16),
            dma((4,)),
            dma((3, 2, half)), dma((3, 2, half)), dma((3, 2, half)), dma((3, 2, half)),
            dma((2,)), dma((2,)),
            dma, dma, dma,
        ],
        compiler_params=pltpu.CompilerParams(
            collective_id=0, has_side_effects=True, vmem_limit_bytes=56 * 1024 * 1024
        ),
    )(inputs, down_weight, up_weight, value_grad)
    return tuple(pl.pallas_call(
        hand_over,
        out_shape=tuple(out(r.shape) for r in results),
        in_specs=[hbm] * 3,
        out_specs=(hbm,) * 3,
        scratch_shapes=[dma((3,))],
    )(*results))


def solution(mesh):
    spec = P("section", "row", "col")
    sizes = (mesh.shape["section"], mesh.shape["row"], mesh.shape["col"])
    return jax.shard_map(
        functools.partial(body, *sizes),
        mesh=mesh,
        in_specs=(spec,) * 4,
        out_specs=(spec,) * 3,
        check_vma=False,
    )
```

```python
import functools

import jax
import jax.numpy as jnp
from jax import lax
from jax.experimental import pallas as pl
from jax.experimental.pallas import tpu as pltpu
from jax.sharding import PartitionSpec as P

DOWN_CUTS = (0, 1)
UP_CUTS = (0, 1, 2)
N_CHAINS = len(DOWN_CUTS) + len(UP_CUTS) - 2
MESH = pl.DeviceIdType.MESH
F32 = jnp.float32
BF16 = jnp.bfloat16


def remote(src, dst, send, recv, device):
    return pltpu.make_async_remote_copy(
        src_ref=src, dst_ref=dst, send_sem=send, recv_sem=recv, device_id=device, device_id_type=MESH
    )


class Stream:
    def __init__(self, **refs):
        self.__dict__.update(refs)


class Chain:
    def __init__(self, stream, index, begin, end):
        self.w, self.s, self.r = stream.w, stream.s, stream.r
        self.left_part, self.right_part = slice(begin, (begin + end) // 2), slice((begin + end) // 2, end)
        self.columns = slice(begin, end)
        self.gather_send, self.gather_recv, self.scatter_send, self.scatter_recv = (
            sem.at[index] for sem in stream.sems
        )


def kernel(n_sec, n_row, n_col, *refs):
    (x_hbm, dw_hbm, uw_hbm, v_hbm, passed_ref, dg_ref, ug_ref) = refs[:7]
    (xs, vs, xt, vt, wd, wu, pd, pu, qd, qu, normed, nb, lb, sd, su, rd, ru, ig, zero, load_sem,
     gather_send, gather_recv, scatter_send, scatter_recv, x_send, x_recv, sec_send, sec_recv, zero_sem) = refs[7:]
    half_ring = n_row // 2
    block = dw_hbm.shape[1]
    latents = n_row * block
    sec, row, col = lax.axis_index("section"), lax.axis_index("row"), lax.axis_index("col")
    right = {"row": lax.rem(row + 1, n_row)}
    left = {"row": lax.rem(row + n_row - 1, n_row)}
    peers = [{"col": lax.rem(col + j, n_col)} for j in range(1, n_col)]
    down = {"section": lax.rem(sec + n_sec - 1, n_sec)}
    up = {"section": lax.rem(sec + 1, n_sec)}

    loads = [
        pltpu.make_async_copy(dw_hbm.at[0], wd.at[0, 0:block], load_sem.at[0]),
        pltpu.make_async_copy(uw_hbm.at[0], wu.at[0, 0:block], load_sem.at[1]),
        pltpu.make_async_copy(x_hbm.at[0], xs, load_sem.at[2]),
        pltpu.make_async_copy(v_hbm.at[0], vs, load_sem.at[3]),
    ]
    for load in loads:
        load.start()
    barrier = pltpu.get_barrier_semaphore()
    for device in [right, left, down, up] + peers:
        pl.semaphore_signal(barrier, inc=1, device_id=device, device_id_type=MESH)
    pl.semaphore_wait(barrier, 4 + len(peers))
    loads[0].wait()
    loads[1].wait()

    sems = (gather_send, gather_recv, scatter_send, scatter_recv)
    d = Stream(w=wd, at=xt, a=xs, p=pd, q=qd, lat=lb, s=sd, r=rd, out=dg_ref, sems=sems,
               x_send=x_send.at[0], x_recv=x_recv.at[0])
    u = Stream(w=wu, at=vt, a=vs, p=pu, q=qu, lat=nb, s=su, r=ru, out=ug_ref, sems=sems,
               x_send=x_send.at[1], x_recv=x_recv.at[1])
    width, feat = xs.shape[1], vs.shape[1]
    for t, cuts in ((d, DOWN_CUTS), (u, UP_CUTS)):
        first = 0 if t is d else len(DOWN_CUTS) - 1
        ends = [t.w.shape[2] * cut // cuts[-1] for cut in cuts]
        t.chains = [Chain(t, first + i, ends[i], ends[i + 1]) for i in range(len(ends) - 1)]
    chains = d.chains + u.chains
    lo, hi = slice(0, block), slice(block, 2 * block)

    def gather_copies(c, k):
        from_hi = lo if isinstance(k, int) and k == 0 else hi
        return (
            remote(c.w.at[k, lo, c.columns], c.w.at[k + 1, lo, c.columns],
                   c.gather_send.at[0, k], c.gather_recv.at[0, k], right),
            remote(c.w.at[k, from_hi, c.columns], c.w.at[k + 1, hi, c.columns],
                   c.gather_send.at[1, k], c.gather_recv.at[1, k], left),
        )

    def gather_last(c):
        k = half_ring - 1
        return (
            remote(c.w.at[k, lo, c.left_part], c.w.at[0, hi, c.left_part],
                   c.gather_send.at[0, k], c.gather_recv.at[0, k], right),
            remote(c.w.at[k, hi, c.right_part], c.w.at[0, hi, c.right_part],
                   c.gather_send.at[1, k], c.gather_recv.at[1, k], left),
        )

    def pass_on(c, k):
        last = isinstance(k, int) and k == half_ring - 1
        for before, after in zip(gather_copies(c, k - 1), gather_last(c) if last else gather_copies(c, k)):
            before.wait_recv()
            after.start()

    def arrive_last(c):
        for copy in gather_last(c):
            copy.wait_recv()

    def partial_latents(t, k):
        t.p[k] = jnp.dot(t.w[k], t.at[...], preferred_element_type=F32).astype(BF16)
        for j, peer in enumerate(peers):
            remote(t.p.at[k], t.q.at[j, k], t.x_send, t.x_recv, peer).start()

    def exchanged(t):
        pltpu.make_async_copy(t.q, t.q, t.x_recv).wait()
        total = t.p[...].astype(F32)
        for j in range(len(peers)):
            total = total + t.q[j].astype(F32)
        return total.reshape(latents, total.shape[-1])

    def scatter_first(c):
        return (
            remote(c.s.at[0, hi, c.left_part], c.r.at[0, hi, c.left_part],
                   c.scatter_send.at[0, 0], c.scatter_recv.at[0, 0], right),
            remote(c.s.at[0, hi, c.right_part], c.r.at[0, lo, c.right_part],
                   c.scatter_send.at[1, 0], c.scatter_recv.at[1, 0], left),
        )

    def scatter_copies(c, j):
        pair = half_ring - j
        return (
            remote(c.s.at[pair, hi, c.columns], c.r.at[j, hi, c.columns],
                   c.scatter_send.at[0, j], c.scatter_recv.at[0, j], right),
            remote(c.s.at[pair, lo, c.columns], c.r.at[j, lo, c.columns],
                   c.scatter_send.at[1, j], c.scatter_recv.at[1, j], left),
        )

    def product(t, pair):
        rows = slice(pair * 2 * block, (pair + 1) * 2 * block)
        t.s[pair] = jnp.dot(t.lat[rows, :], t.a[...], preferred_element_type=F32).astype(BF16)

    def scatter_start(t):
        product(t, 0)
        for c in t.chains:
            for copy in scatter_first(c):
                copy.start()

    def scatter_step(t, j):
        pair = half_ring - j
        product(t, pair)
        for c in t.chains:
            arrived = scatter_first(c) if j == 1 else scatter_copies(c, j - 1)
            for part, before, after in zip((hi, lo), arrived, scatter_copies(c, j)):
                before.wait_recv()
                t.s[pair, part, c.columns] = (
                    t.s[pair, part, c.columns].astype(F32) + t.r[j - 1, part, c.columns].astype(F32)
                ).astype(BF16)
                after.start()

    def scatter_end(t):
        last = half_ring - 1
        for c in t.chains:
            for copy in scatter_copies(c, last):
                copy.wait_recv()
        t.out[0] = (
            t.s[0, lo].astype(F32) + t.r[last, lo].astype(F32) + t.r[last, hi].astype(F32)
        ).astype(BF16)

    for c in chains:
        for copy in gather_copies(c, 0):
            copy.start()
    for c in chains:
        c.r[0, lo, c.left_part] = jnp.zeros((block, c.left_part.stop - c.left_part.start), BF16)
        c.r[0, hi, c.right_part] = jnp.zeros((block, c.right_part.stop - c.right_part.start), BF16)
    zero[...] = jnp.zeros_like(zero)
    loads[2].wait()
    xt[...] = xs[...].T
    loads[3].wait()
    vt[...] = vs[...].T

    @pl.loop(1, half_ring - 1)
    def _(k):
        for t in (d, u):
            for c in t.chains:
                pass_on(c, k)
            partial_latents(t, k)

    for t in (d, u):
        for c in t.chains:
            pass_on(c, half_ring - 1)
        partial_latents(t, half_ring - 1)
    for t in (d, u):
        for c in t.chains:
            arrive_last(c)
        partial_latents(t, 0)

    latent = exchanged(d)
    inv_rms = lax.rsqrt(jnp.sum(latent * latent, axis=0, keepdims=True) * (1.0 / latents) + 1e-6)
    value = latent * inv_rms
    nb[...] = value.astype(BF16)
    normed[...] = value
    scatter_start(u)

    normed_grad = exchanged(u)
    value = normed[...]
    inner = jnp.sum(normed_grad * value, axis=0, keepdims=True) * (1.0 / latents)
    lat_grad = inv_rms * (normed_grad - value * inner)
    lb[...] = lat_grad.astype(BF16)
    scatter_start(d)

    scatter_step(u, 1)
    scatter_step(d, 1)

    ig[...] = jnp.dot(
        lb[...].T, wd[...].reshape(latents, width), preferred_element_type=F32
    ).astype(BF16)
    to_section = remote(ig, passed_ref.at[0], sec_send, sec_recv, down)
    fill = pltpu.make_async_copy(zero, passed_ref.at[0], zero_sem)

    @pl.when(sec > 0)
    def _():
        to_section.start()

    @pl.when(sec == n_sec - 1)
    def _():
        fill.start()

    for j in range(2, half_ring):
        scatter_step(u, j)
        scatter_step(d, j)

    scatter_end(u)
    scatter_end(d)

    @pl.when(sec > 0)
    def _():
        to_section.wait_send()

    @pl.when(sec < n_sec - 1)
    def _():
        to_section.wait_recv()

    @pl.when(sec == n_sec - 1)
    def _():
        fill.wait()

    for t in (d, u):
        pltpu.make_async_copy(t.q, t.q, t.x_send).wait()
    for c in chains:
        for copy in gather_copies(c, 0) + gather_last(c) + scatter_first(c):
            copy.wait_send()

        @pl.loop(1, half_ring - 1)
        def _(k):
            for copy in gather_copies(c, k):
                copy.wait_send()

        @pl.loop(1, half_ring)
        def _(j):
            for copy in scatter_copies(c, j):
                copy.wait_send()


def hand_over(*refs):
    results, outs, held, (in_sem, out_sem) = refs[0:3], refs[3:6], refs[6:9], refs[9:]
    reads = [pltpu.make_async_copy(results[i], held[i], in_sem.at[i]) for i in range(3)]
    writes = [pltpu.make_async_copy(held[i], outs[i], out_sem.at[i]) for i in range(3)]
    for read in reads:
        read.start()
    for read, write in zip(reads, writes):
        read.wait()
        write.start()
    for write in writes:
        write.wait()


def body(n_sec, n_row, n_col, inputs, down_weight, up_weight, value_grad):
    _, tokens, width = inputs.shape
    _, block, feat = up_weight.shape
    half = n_row // 2
    latents = n_row * block
    pair = 2 * block
    dma = pltpu.SemaphoreType.DMA
    out = lambda shape: jax.ShapeDtypeStruct(shape, BF16)
    hbm = pl.BlockSpec(memory_space=pltpu.HBM)
    results = pl.pallas_call(
        functools.partial(kernel, n_sec, n_row, n_col),
        out_shape=(out(inputs.shape), out(down_weight.shape), out(up_weight.shape)),
        in_specs=[hbm] * 4,
        out_specs=(
            hbm,
            pl.BlockSpec(memory_space=pltpu.VMEM),
            pl.BlockSpec(memory_space=pltpu.VMEM),
        ),
        scratch_shapes=[
            pltpu.VMEM((tokens, width), BF16),
            pltpu.VMEM((tokens, feat), BF16),
            pltpu.VMEM((width, tokens), BF16),
            pltpu.VMEM((feat, tokens), BF16),
            pltpu.VMEM((half, pair, width), BF16),
            pltpu.VMEM((half, pair, feat), BF16),
            pltpu.VMEM((half, pair, tokens), BF16),
            pltpu.VMEM((half, pair, tokens), BF16),
            pltpu.VMEM((n_col - 1, half, pair, tokens), BF16),
            pltpu.VMEM((n_col - 1, half, pair, tokens), BF16),
            pltpu.VMEM((latents, tokens), F32),
            pltpu.VMEM((latents, tokens), BF16),
            pltpu.VMEM((latents, tokens), BF16),
            pltpu.VMEM((half, pair, width), BF16),
            pltpu.VMEM((half, pair, feat), BF16),
            pltpu.VMEM((half, pair, width), BF16),
            pltpu.VMEM((half, pair, feat), BF16),
            pltpu.VMEM((tokens, width), BF16),
            pltpu.VMEM((tokens, width), BF16),
            dma((4,)),
            dma((N_CHAINS, 2, half)), dma((N_CHAINS, 2, half)), dma((N_CHAINS, 2, half)), dma((N_CHAINS, 2, half)),
            dma((2,)), dma((2,)),
            dma, dma, dma,
        ],
        compiler_params=pltpu.CompilerParams(
            collective_id=0, has_side_effects=True, vmem_limit_bytes=56 * 1024 * 1024
        ),
    )(inputs, down_weight, up_weight, value_grad)
    return tuple(pl.pallas_call(
        hand_over,
        out_shape=tuple(out(r.shape) for r in results),
        in_specs=[hbm] * 3,
        out_specs=(hbm,) * 3,
        scratch_shapes=[pltpu.VMEM(r.shape, BF16) for r in results] + [dma((3,)), dma((3,))],
    )(*results))


def solution(mesh):
    spec = P("section", "row", "col")
    sizes = (mesh.shape["section"], mesh.shape["row"], mesh.shape["col"])
    return jax.shard_map(
        functools.partial(body, *sizes),
        mesh=mesh,
        in_specs=(spec,) * 4,
        out_specs=(spec,) * 3,
        check_vma=False,
    )
```

```python
import functools

import jax
import jax.numpy as jnp
from jax import lax
from jax.experimental import pallas as pl
from jax.experimental.pallas import tpu as pltpu
from jax.sharding import PartitionSpec as P

DOWN_CUTS = (0, 1)
UP_CUTS = (0, 1, 2)
N_CHAINS = len(DOWN_CUTS) + len(UP_CUTS) - 2
MESH = pl.DeviceIdType.MESH
F32 = jnp.float32
BF16 = jnp.bfloat16


def remote(src, dst, send, recv, device):
    return pltpu.make_async_remote_copy(
        src_ref=src, dst_ref=dst, send_sem=send, recv_sem=recv, device_id=device, device_id_type=MESH
    )


class Stream:
    def __init__(self, **refs):
        self.__dict__.update(refs)


class Chain:
    def __init__(self, stream, index, begin, end):
        self.w, self.s, self.r = stream.w, stream.s, stream.r
        self.left_part, self.right_part = slice(begin, (begin + end) // 2), slice((begin + end) // 2, end)
        self.columns = slice(begin, end)
        self.gather_send, self.gather_recv, self.scatter_send, self.scatter_recv = (
            sem.at[index] for sem in stream.sems
        )


def kernel(n_sec, n_row, n_col, *refs):
    (x_hbm, dw_hbm, uw_hbm, v_hbm, passed_ref, dg_ref, ug_ref) = refs[:7]
    (xs, vs, xt, vt, wd, wu, pd, pu, qd, qu, normed, grads, nb, lb, sd, su, rd, ru, ig, load_sem,
     gather_send, gather_recv, scatter_send, scatter_recv, x_send, x_recv, sec_send, sec_recv) = refs[7:]
    half_ring = n_row // 2
    block = dw_hbm.shape[1]
    latents = n_row * block
    sec, row, col = lax.axis_index("section"), lax.axis_index("row"), lax.axis_index("col")
    right = {"row": lax.rem(row + 1, n_row)}
    left = {"row": lax.rem(row + n_row - 1, n_row)}
    peers = [{"col": lax.rem(col + j, n_col)} for j in range(1, n_col)]
    down = {"section": lax.rem(sec + n_sec - 1, n_sec)}
    up = {"section": lax.rem(sec + 1, n_sec)}

    loads = [
        pltpu.make_async_copy(dw_hbm.at[0], wd.at[0, 0:block], load_sem.at[0]),
        pltpu.make_async_copy(uw_hbm.at[0], wu.at[0, 0:block], load_sem.at[1]),
        pltpu.make_async_copy(x_hbm.at[0], xs, load_sem.at[2]),
        pltpu.make_async_copy(v_hbm.at[0], vs, load_sem.at[3]),
    ]
    for load in loads:
        load.start()
    barrier = pltpu.get_barrier_semaphore()
    for device in [right, left, down, up] + peers:
        pl.semaphore_signal(barrier, inc=1, device_id=device, device_id_type=MESH)
    pl.semaphore_wait(barrier, 4 + len(peers))
    loads[0].wait()
    loads[1].wait()

    sems = (gather_send, gather_recv, scatter_send, scatter_recv)
    d = Stream(w=wd, at=xt, a=xs, p=pd, q=qd, lat=lb, s=sd, r=rd, out=dg_ref, sems=sems,
               x_send=x_send.at[0], x_recv=x_recv.at[0])
    u = Stream(w=wu, at=vt, a=vs, p=pu, q=qu, lat=nb, s=su, r=ru, out=ug_ref, sems=sems,
               x_send=x_send.at[1], x_recv=x_recv.at[1])
    width, feat = xs.shape[1], vs.shape[1]
    for t, cuts in ((d, DOWN_CUTS), (u, UP_CUTS)):
        first = 0 if t is d else len(DOWN_CUTS) - 1
        ends = [t.w.shape[2] * cut // cuts[-1] for cut in cuts]
        t.chains = [Chain(t, first + i, ends[i], ends[i + 1]) for i in range(len(ends) - 1)]
    chains = d.chains + u.chains
    lo, hi = slice(0, block), slice(block, 2 * block)

    def gather_copies(c, k):
        from_hi = lo if isinstance(k, int) and k == 0 else hi
        return (
            remote(c.w.at[k, lo, c.columns], c.w.at[k + 1, lo, c.columns],
                   c.gather_send.at[0, k], c.gather_recv.at[0, k], right),
            remote(c.w.at[k, from_hi, c.columns], c.w.at[k + 1, hi, c.columns],
                   c.gather_send.at[1, k], c.gather_recv.at[1, k], left),
        )

    def gather_last(c):
        k = half_ring - 1
        return (
            remote(c.w.at[k, lo, c.left_part], c.w.at[0, hi, c.left_part],
                   c.gather_send.at[0, k], c.gather_recv.at[0, k], right),
            remote(c.w.at[k, hi, c.right_part], c.w.at[0, hi, c.right_part],
                   c.gather_send.at[1, k], c.gather_recv.at[1, k], left),
        )

    def pass_on(c, k):
        last = isinstance(k, int) and k == half_ring - 1
        for before, after in zip(gather_copies(c, k - 1), gather_last(c) if last else gather_copies(c, k)):
            before.wait_recv()
            after.start()

    def arrive_last(c):
        for copy in gather_last(c):
            copy.wait_recv()

    def partial_latents(t, k):
        t.p[k] = jnp.dot(t.w[k], t.at[...], preferred_element_type=F32).astype(BF16)
        for j, peer in enumerate(peers):
            last = isinstance(k, int) and k == 0
            remote(t.p.at[k], t.q.at[j, k], t.x_send, t.x_recv.at[1 if last else 0], peer).start()

    def exchanged(t, pairs, sem):
        arrived = t.q.at[:, pairs]
        pltpu.make_async_copy(arrived, arrived, t.x_recv.at[sem]).wait()
        total = t.p[pairs].astype(F32)
        for j in range(len(peers)):
            total = total + t.q[j, pairs].astype(F32)
        return total.reshape(-1, total.shape[-1])

    def scatter_first(c):
        return (
            remote(c.s.at[0, hi, c.left_part], c.r.at[0, hi, c.left_part],
                   c.scatter_send.at[0, 0], c.scatter_recv.at[0, 0], right),
            remote(c.s.at[0, hi, c.right_part], c.r.at[0, lo, c.right_part],
                   c.scatter_send.at[1, 0], c.scatter_recv.at[1, 0], left),
        )

    def scatter_copies(c, j):
        pair = half_ring - j
        return (
            remote(c.s.at[pair, hi, c.columns], c.r.at[j, hi, c.columns],
                   c.scatter_send.at[0, j], c.scatter_recv.at[0, j], right),
            remote(c.s.at[pair, lo, c.columns], c.r.at[j, lo, c.columns],
                   c.scatter_send.at[1, j], c.scatter_recv.at[1, j], left),
        )

    def product(t, pair):
        rows = slice(pair * 2 * block, (pair + 1) * 2 * block)
        t.s[pair] = jnp.dot(t.lat[rows, :], t.a[...], preferred_element_type=F32).astype(BF16)

    def scatter_start(t):
        product(t, 0)
        for c in t.chains:
            for copy in scatter_first(c):
                copy.start()

    def scatter_step(t, j):
        pair = half_ring - j
        product(t, pair)
        for c in t.chains:
            arrived = scatter_first(c) if j == 1 else scatter_copies(c, j - 1)
            for part, before, after in zip((hi, lo), arrived, scatter_copies(c, j)):
                before.wait_recv()
                t.s[pair, part, c.columns] = (
                    t.s[pair, part, c.columns].astype(F32) + t.r[j - 1, part, c.columns].astype(F32)
                ).astype(BF16)
                after.start()

    def scatter_end(t):
        last = half_ring - 1
        for c in t.chains:
            for copy in scatter_copies(c, last):
                copy.wait_recv()
        t.out[0] = (
            t.s[0, lo].astype(F32) + t.r[last, lo].astype(F32) + t.r[last, hi].astype(F32)
        ).astype(BF16)

    for c in chains:
        for copy in gather_copies(c, 0):
            copy.start()
    for c in chains:
        c.r[0, lo, c.left_part] = jnp.zeros((block, c.left_part.stop - c.left_part.start), BF16)
        c.r[0, hi, c.right_part] = jnp.zeros((block, c.right_part.stop - c.right_part.start), BF16)
    loads[2].wait()
    xt[...] = xs[...].T
    loads[3].wait()
    vt[...] = vs[...].T

    @pl.loop(1, half_ring - 1)
    def _(k):
        for t in (d, u):
            for c in t.chains:
                pass_on(c, k)
            partial_latents(t, k)

    for t in (d, u):
        for c in t.chains:
            pass_on(c, half_ring - 1)
        partial_latents(t, half_ring - 1)
    early, final = slice(1, half_ring), slice(0, 1)
    head, rest = slice(0, 2 * block), slice(2 * block, latents)

    def total_of(value):
        return jnp.sum(value, axis=0, keepdims=True)

    for c in d.chains:
        arrive_last(c)
    partial_latents(d, 0)
    latent_early = exchanged(d, early, 0)
    normed[rest, :] = latent_early
    squares = total_of(latent_early * latent_early)
    for c in u.chains:
        arrive_last(c)
    partial_latents(u, 0)

    latent_final = exchanged(d, final, 1)
    inv_rms = lax.rsqrt((squares + total_of(latent_final * latent_final)) * (1.0 / latents) + 1e-6)
    value_final = latent_final * inv_rms
    nb[head, :] = value_final.astype(BF16)
    scatter_start(u)
    value = normed[rest, :] * inv_rms
    nb[rest, :] = value.astype(BF16)
    normed[rest, :] = value

    grad_early = exchanged(u, early, 0)
    grads[rest, :] = grad_early
    inner = total_of(grad_early * value)
    grad_final = exchanged(u, final, 1)
    inner = (inner + total_of(grad_final * value_final)) * (1.0 / latents)
    lb[head, :] = (inv_rms * (grad_final - value_final * inner)).astype(BF16)
    scatter_start(d)
    lb[rest, :] = (inv_rms * (grads[rest, :] - normed[rest, :] * inner)).astype(BF16)

    scatter_step(u, 1)
    scatter_step(d, 1)

    ig[...] = jnp.dot(
        lb[...].T, wd[...].reshape(latents, width), preferred_element_type=F32
    ).astype(BF16)
    to_section = remote(ig, passed_ref.at[0], sec_send, sec_recv, down)

    @pl.when(sec > 0)
    def _():
        to_section.start()

    @pl.when(sec == n_sec - 1)
    def _():
        passed_ref[...] = jnp.zeros_like(passed_ref)

    for j in range(2, half_ring):
        scatter_step(u, j)
        scatter_step(d, j)

    scatter_end(u)
    scatter_end(d)

    @pl.when(sec > 0)
    def _():
        to_section.wait_send()

    @pl.when(sec < n_sec - 1)
    def _():
        to_section.wait_recv()

    for t in (d, u):
        pltpu.make_async_copy(t.q, t.q, t.x_send).wait()
    for c in chains:
        for copy in gather_copies(c, 0) + gather_last(c) + scatter_first(c):
            copy.wait_send()

        @pl.loop(1, half_ring - 1)
        def _(k):
            for copy in gather_copies(c, k):
                copy.wait_send()

        @pl.loop(1, half_ring)
        def _(j):
            for copy in scatter_copies(c, j):
                copy.wait_send()


def hand_over(*refs):
    copies = [pltpu.make_async_copy(refs[i], refs[3 + i], refs[6].at[i]) for i in range(3)]
    for copy in copies:
        copy.start()
    for copy in copies:
        copy.wait()


def body(n_sec, n_row, n_col, inputs, down_weight, up_weight, value_grad):
    _, tokens, width = inputs.shape
    _, block, feat = up_weight.shape
    half = n_row // 2
    latents = n_row * block
    pair = 2 * block
    dma = pltpu.SemaphoreType.DMA
    out = lambda shape: jax.ShapeDtypeStruct(shape, BF16)
    hbm = pl.BlockSpec(memory_space=pltpu.HBM)
    results = pl.pallas_call(
        functools.partial(kernel, n_sec, n_row, n_col),
        out_shape=(out(inputs.shape), out(down_weight.shape), out(up_weight.shape)),
        in_specs=[hbm] * 4,
        out_specs=(
            pl.BlockSpec(memory_space=pltpu.VMEM),
            pl.BlockSpec(memory_space=pltpu.VMEM),
            pl.BlockSpec(memory_space=pltpu.VMEM),
        ),
        scratch_shapes=[
            pltpu.VMEM((tokens, width), BF16),
            pltpu.VMEM((tokens, feat), BF16),
            pltpu.VMEM((width, tokens), BF16),
            pltpu.VMEM((feat, tokens), BF16),
            pltpu.VMEM((half, pair, width), BF16),
            pltpu.VMEM((half, pair, feat), BF16),
            pltpu.VMEM((half, pair, tokens), BF16),
            pltpu.VMEM((half, pair, tokens), BF16),
            pltpu.VMEM((n_col - 1, half, pair, tokens), BF16),
            pltpu.VMEM((n_col - 1, half, pair, tokens), BF16),
            pltpu.VMEM((latents, tokens), F32),
            pltpu.VMEM((latents, tokens), F32),
            pltpu.VMEM((latents, tokens), BF16),
            pltpu.VMEM((latents, tokens), BF16),
            pltpu.VMEM((half, pair, width), BF16),
            pltpu.VMEM((half, pair, feat), BF16),
            pltpu.VMEM((half, pair, width), BF16),
            pltpu.VMEM((half, pair, feat), BF16),
            pltpu.VMEM((tokens, width), BF16),
            dma((4,)),
            dma((N_CHAINS, 2, half)), dma((N_CHAINS, 2, half)), dma((N_CHAINS, 2, half)), dma((N_CHAINS, 2, half)),
            dma((2,)), dma((2, 2)),
            dma, dma,
        ],
        compiler_params=pltpu.CompilerParams(
            collective_id=0, has_side_effects=True, vmem_limit_bytes=40 * 1024 * 1024
        ),
    )(*(pltpu.with_memory_space_constraint(a, pltpu.HBM) for a in (inputs, down_weight, up_weight, value_grad)))
    return tuple(pl.pallas_call(
        hand_over,
        out_shape=tuple(out(r.shape) for r in results),
        in_specs=[pl.BlockSpec(memory_space=pltpu.VMEM)] * 3,
        out_specs=(hbm,) * 3,
        scratch_shapes=[dma((3,))],
    )(*(pltpu.with_memory_space_constraint(r, pltpu.VMEM) for r in results)))


def solution(mesh):
    spec = P("section", "row", "col")
    sizes = (mesh.shape["section"], mesh.shape["row"], mesh.shape["col"])
    return jax.shard_map(
        functools.partial(body, *sizes),
        mesh=mesh,
        in_specs=(spec,) * 4,
        out_specs=(spec,) * 3,
        check_vma=False,
    )
```

```python
import functools

import jax
import jax.numpy as jnp
from jax import lax
from jax.experimental import pallas as pl
from jax.experimental.pallas import tpu as pltpu
from jax.sharding import PartitionSpec as P

DOWN_CUTS = (0, 1)
UP_CUTS = (0, 1, 2)
N_CHAINS = len(DOWN_CUTS) + len(UP_CUTS) - 2
MESH = pl.DeviceIdType.MESH
F32 = jnp.float32
BF16 = jnp.bfloat16


def remote(src, dst, send, recv, device):
    return pltpu.make_async_remote_copy(
        src_ref=src, dst_ref=dst, send_sem=send, recv_sem=recv, device_id=device, device_id_type=MESH
    )


class Stream:
    def __init__(self, **refs):
        self.__dict__.update(refs)


class Chain:
    def __init__(self, stream, index, begin, end):
        self.w, self.s, self.r = stream.w, stream.s, stream.r
        self.left_part, self.right_part = slice(begin, (begin + end) // 2), slice((begin + end) // 2, end)
        self.columns = slice(begin, end)
        self.gather_send, self.gather_recv, self.scatter_send, self.scatter_recv = (
            sem.at[index] for sem in stream.sems
        )


def kernel(n_sec, n_row, n_col, *refs):
    (x_hbm, dw_hbm, uw_hbm, v_hbm, passed_ref, dg_ref, ug_ref) = refs[:7]
    (xs, vs, xt, vt, wd, wu, pd, pu, qd, qu, normed, grads, nb, lb, sd, su, rd, ru, ig, load_sem,
     gather_send, gather_recv, scatter_send, scatter_recv, x_send, x_recv, sec_send, sec_recv) = refs[7:]
    half_ring = n_row // 2
    block = dw_hbm.shape[1]
    latents = n_row * block
    sec, row, col = lax.axis_index("section"), lax.axis_index("row"), lax.axis_index("col")
    right = {"row": lax.rem(row + 1, n_row)}
    left = {"row": lax.rem(row + n_row - 1, n_row)}
    peers = [{"col": lax.rem(col + j, n_col)} for j in range(1, n_col)]
    down = {"section": lax.rem(sec + n_sec - 1, n_sec)}
    up = {"section": lax.rem(sec + 1, n_sec)}

    loads = [
        pltpu.make_async_copy(dw_hbm.at[0], wd.at[0, 0:block], load_sem.at[0]),
        pltpu.make_async_copy(uw_hbm.at[0], wu.at[0, 0:block], load_sem.at[1]),
        pltpu.make_async_copy(x_hbm.at[0], xs, load_sem.at[2]),
        pltpu.make_async_copy(v_hbm.at[0], vs, load_sem.at[3]),
    ]
    for load in loads:
        load.start()
    barrier = pltpu.get_barrier_semaphore()
    for device in [right, left] + peers:
        pl.semaphore_signal(barrier, inc=1, device_id=device, device_id_type=MESH)

    @pl.when(sec < n_sec - 1)
    def _():
        pl.semaphore_signal(barrier, inc=1, device_id=up, device_id_type=MESH)

    pl.semaphore_wait(barrier, 2 + len(peers) + lax.div(sec + n_sec - 1, n_sec))
    loads[0].wait()
    loads[1].wait()

    sems = (gather_send, gather_recv, scatter_send, scatter_recv)
    d = Stream(w=wd, at=xt, a=xs, p=pd, q=qd, lat=lb, s=sd, r=rd, out=dg_ref, sems=sems,
               x_send=x_send.at[0], x_recv=x_recv.at[0])
    u = Stream(w=wu, at=vt, a=vs, p=pu, q=qu, lat=nb, s=su, r=ru, out=ug_ref, sems=sems,
               x_send=x_send.at[1], x_recv=x_recv.at[1])
    width, feat = xs.shape[1], vs.shape[1]
    for t, cuts in ((d, DOWN_CUTS), (u, UP_CUTS)):
        first = 0 if t is d else len(DOWN_CUTS) - 1
        ends = [t.w.shape[2] * cut // cuts[-1] for cut in cuts]
        t.chains = [Chain(t, first + i, ends[i], ends[i + 1]) for i in range(len(ends) - 1)]
    chains = d.chains + u.chains
    lo, hi = slice(0, block), slice(block, 2 * block)

    def gather_copies(c, k):
        from_hi = lo if isinstance(k, int) and k == 0 else hi
        return (
            remote(c.w.at[k, lo, c.columns], c.w.at[k + 1, lo, c.columns],
                   c.gather_send.at[0, k], c.gather_recv.at[0, k], right),
            remote(c.w.at[k, from_hi, c.columns], c.w.at[k + 1, hi, c.columns],
                   c.gather_send.at[1, k], c.gather_recv.at[1, k], left),
        )

    def gather_last(c):
        k = half_ring - 1
        return (
            remote(c.w.at[k, lo, c.left_part], c.w.at[0, hi, c.left_part],
                   c.gather_send.at[0, k], c.gather_recv.at[0, k], right),
            remote(c.w.at[k, hi, c.right_part], c.w.at[0, hi, c.right_part],
                   c.gather_send.at[1, k], c.gather_recv.at[1, k], left),
        )

    def pass_on(c, k):
        last = isinstance(k, int) and k == half_ring - 1
        for before, after in zip(gather_copies(c, k - 1), gather_last(c) if last else gather_copies(c, k)):
            before.wait_recv()
            after.start()

    def arrive_last(c):
        for copy in gather_last(c):
            copy.wait_recv()

    def partial_latents(t, k):
        t.p[k] = jnp.dot(t.w[k], t.at[...], preferred_element_type=F32).astype(BF16)
        for j, peer in enumerate(peers):
            last = isinstance(k, int) and k == 0
            remote(t.p.at[k], t.q.at[j, k], t.x_send, t.x_recv.at[1 if last else 0], peer).start()

    def exchanged(t, pairs, sem):
        arrived = t.q.at[:, pairs]
        pltpu.make_async_copy(arrived, arrived, t.x_recv.at[sem]).wait()
        total = t.p[pairs].astype(F32)
        for j in range(len(peers)):
            total = total + t.q[j, pairs].astype(F32)
        return total.reshape(-1, total.shape[-1])

    def scatter_first(c):
        return (
            remote(c.s.at[0, hi, c.left_part], c.r.at[0, hi, c.left_part],
                   c.scatter_send.at[0, 0], c.scatter_recv.at[0, 0], right),
            remote(c.s.at[0, hi, c.right_part], c.r.at[0, lo, c.right_part],
                   c.scatter_send.at[1, 0], c.scatter_recv.at[1, 0], left),
        )

    def scatter_copies(c, j):
        pair = half_ring - j
        return (
            remote(c.s.at[pair, hi, c.columns], c.r.at[j, hi, c.columns],
                   c.scatter_send.at[0, j], c.scatter_recv.at[0, j], right),
            remote(c.s.at[pair, lo, c.columns], c.r.at[j, lo, c.columns],
                   c.scatter_send.at[1, j], c.scatter_recv.at[1, j], left),
        )

    def product(t, pair):
        rows = slice(pair * 2 * block, (pair + 1) * 2 * block)
        t.s[pair] = jnp.dot(t.lat[rows, :], t.a[...], preferred_element_type=F32).astype(BF16)

    def scatter_start(t):
        product(t, 0)
        for c in t.chains:
            for copy in scatter_first(c):
                copy.start()

    def scatter_step(t, j):
        pair = half_ring - j
        product(t, pair)
        for c in t.chains:
            arrived = scatter_first(c) if j == 1 else scatter_copies(c, j - 1)
            for part, before, after in zip((hi, lo), arrived, scatter_copies(c, j)):
                before.wait_recv()
                t.s[pair, part, c.columns] = (
                    t.s[pair, part, c.columns].astype(F32) + t.r[j - 1, part, c.columns].astype(F32)
                ).astype(BF16)
                after.start()

    def scatter_end(t):
        last = half_ring - 1
        for c in t.chains:
            for copy in scatter_copies(c, last):
                copy.wait_recv()
        t.out[0] = (
            t.s[0, lo].astype(F32) + t.r[last, lo].astype(F32) + t.r[last, hi].astype(F32)
        ).astype(BF16)

    for c in chains:
        for copy in gather_copies(c, 0):
            copy.start()
    for c in chains:
        c.r[0, lo, c.left_part] = jnp.zeros((block, c.left_part.stop - c.left_part.start), BF16)
        c.r[0, hi, c.right_part] = jnp.zeros((block, c.right_part.stop - c.right_part.start), BF16)
    loads[2].wait()
    xt[...] = xs[...].T
    loads[3].wait()
    vt[...] = vs[...].T

    @pl.loop(1, half_ring - 1)
    def _(k):
        for t in (d, u):
            for c in t.chains:
                pass_on(c, k)
            partial_latents(t, k)

    for t in (d, u):
        for c in t.chains:
            pass_on(c, half_ring - 1)
        partial_latents(t, half_ring - 1)
    early, final = slice(1, half_ring), slice(0, 1)
    head, rest = slice(0, 2 * block), slice(2 * block, latents)

    def total_of(value):
        return jnp.sum(value, axis=0, keepdims=True)

    for c in d.chains:
        arrive_last(c)
    partial_latents(d, 0)
    latent_early = exchanged(d, early, 0)
    normed[rest, :] = latent_early
    squares = total_of(latent_early * latent_early)
    for c in u.chains:
        arrive_last(c)
    partial_latents(u, 0)

    latent_final = exchanged(d, final, 1)
    inv_rms = lax.rsqrt((squares + total_of(latent_final * latent_final)) * (1.0 / latents) + 1e-6)
    value_final = latent_final * inv_rms
    nb[head, :] = value_final.astype(BF16)
    scatter_start(u)
    value = normed[rest, :] * inv_rms
    nb[rest, :] = value.astype(BF16)
    normed[rest, :] = value

    grad_early = exchanged(u, early, 0)
    grads[rest, :] = grad_early
    inner = total_of(grad_early * value)
    grad_final = exchanged(u, final, 1)
    inner = (inner + total_of(grad_final * value_final)) * (1.0 / latents)
    lb[head, :] = (inv_rms * (grad_final - value_final * inner)).astype(BF16)
    scatter_start(d)
    lb[rest, :] = (inv_rms * (grads[rest, :] - normed[rest, :] * inner)).astype(BF16)

    scatter_step(u, 1)
    scatter_step(d, 1)

    ig[...] = jnp.dot(
        lb[...].T, wd[...].reshape(latents, width), preferred_element_type=F32
    ).astype(BF16)
    to_section = remote(ig, passed_ref.at[0], sec_send, sec_recv, down)

    @pl.when(sec > 0)
    def _():
        to_section.start()

    @pl.when(sec == n_sec - 1)
    def _():
        passed_ref[...] = jnp.zeros_like(passed_ref)

    for j in range(2, half_ring):
        scatter_step(u, j)
        scatter_step(d, j)

    scatter_end(u)
    scatter_end(d)

    @pl.when(sec > 0)
    def _():
        to_section.wait_send()

    @pl.when(sec < n_sec - 1)
    def _():
        to_section.wait_recv()

    for t in (d, u):
        pltpu.make_async_copy(t.q, t.q, t.x_send).wait()
    for c in chains:
        for copy in gather_copies(c, 0) + gather_last(c) + scatter_first(c):
            copy.wait_send()

        @pl.loop(1, half_ring - 1)
        def _(k):
            for copy in gather_copies(c, k):
                copy.wait_send()

        @pl.loop(1, half_ring)
        def _(j):
            for copy in scatter_copies(c, j):
                copy.wait_send()


def hand_over(*refs):
    copies = [pltpu.make_async_copy(refs[i], refs[3 + i], refs[6].at[i]) for i in range(3)]
    for copy in copies:
        copy.start()
    for copy in copies:
        copy.wait()


def body(n_sec, n_row, n_col, inputs, down_weight, up_weight, value_grad):
    _, tokens, width = inputs.shape
    _, block, feat = up_weight.shape
    half = n_row // 2
    latents = n_row * block
    pair = 2 * block
    dma = pltpu.SemaphoreType.DMA
    out = lambda shape: jax.ShapeDtypeStruct(shape, BF16)
    hbm = pl.BlockSpec(memory_space=pltpu.HBM)
    results = pl.pallas_call(
        functools.partial(kernel, n_sec, n_row, n_col),
        out_shape=(out(inputs.shape), out(down_weight.shape), out(up_weight.shape)),
        in_specs=[hbm] * 4,
        out_specs=(
            pl.BlockSpec(memory_space=pltpu.VMEM),
            pl.BlockSpec(memory_space=pltpu.VMEM),
            pl.BlockSpec(memory_space=pltpu.VMEM),
        ),
        scratch_shapes=[
            pltpu.VMEM((tokens, width), BF16),
            pltpu.VMEM((tokens, feat), BF16),
            pltpu.VMEM((width, tokens), BF16),
            pltpu.VMEM((feat, tokens), BF16),
            pltpu.VMEM((half, pair, width), BF16),
            pltpu.VMEM((half, pair, feat), BF16),
            pltpu.VMEM((half, pair, tokens), BF16),
            pltpu.VMEM((half, pair, tokens), BF16),
            pltpu.VMEM((n_col - 1, half, pair, tokens), BF16),
            pltpu.VMEM((n_col - 1, half, pair, tokens), BF16),
            pltpu.VMEM((latents, tokens), F32),
            pltpu.VMEM((latents, tokens), F32),
            pltpu.VMEM((latents, tokens), BF16),
            pltpu.VMEM((latents, tokens), BF16),
            pltpu.VMEM((half, pair, width), BF16),
            pltpu.VMEM((half, pair, feat), BF16),
            pltpu.VMEM((half, pair, width), BF16),
            pltpu.VMEM((half, pair, feat), BF16),
            pltpu.VMEM((tokens, width), BF16),
            dma((4,)),
            dma((N_CHAINS, 2, half)), dma((N_CHAINS, 2, half)), dma((N_CHAINS, 2, half)), dma((N_CHAINS, 2, half)),
            dma((2,)), dma((2, 2)),
            dma, dma,
        ],
        compiler_params=pltpu.CompilerParams(
            collective_id=0, has_side_effects=True, vmem_limit_bytes=40 * 1024 * 1024
        ),
    )(*(pltpu.with_memory_space_constraint(a, pltpu.HBM) for a in (inputs, down_weight, up_weight, value_grad)))
    return tuple(pl.pallas_call(
        hand_over,
        out_shape=tuple(out(r.shape) for r in results),
        in_specs=[pl.BlockSpec(memory_space=pltpu.VMEM)] * 3,
        out_specs=(hbm,) * 3,
        scratch_shapes=[dma((3,))],
    )(*(pltpu.with_memory_space_constraint(r, pltpu.VMEM) for r in results)))


def solution(mesh):
    spec = P("section", "row", "col")
    sizes = (mesh.shape["section"], mesh.shape["row"], mesh.shape["col"])
    return jax.shard_map(
        functools.partial(body, *sizes),
        mesh=mesh,
        in_specs=(spec,) * 4,
        out_specs=(spec,) * 3,
        check_vma=False,
    )
```
